32 devices in a mesh: freq: 4 (over z), row: 4 (over y, x), col: 2 (over core).
Axes of the slice: x: 2, y: 2, z: 4, core: 2. Of those that a mesh axis runs over, the one named last changes fastest.
Arguments:
- prior_factor: bfloat16 [4, 26624, 1024], P('freq', ('row', 'col')), may hold values from -1 to 1, as said below
- prior_seeds: int32 [4, 26624, 512], P('freq', ('row', 'col')), may hold values from 0 to 4095
- window_seeds: int32 [4, 1024, 512], P('freq'), may hold values from 0 to 4095
- spectra: float32 [4, 1024], P('freq'), may hold values from 0.25 to 1
- nugget: float32 [4, 1024], P('freq'), may hold values from 0.6 to 1.2
- decay: float32 [4], P('freq'), may hold values from 0.2 to 2
Outputs:
- velocity: float32 [512, 1024, 256], P('freq', ('row', 'col'))
The draws below stay inside these ranges and needn't reach their ends.
Inputs may be any that keep to these rules, and one draw needn't show every extreme that they name: `prior_factor`: every entry is smaller in magnitude than 0.95 / (sqrt(26624) + sqrt(1024)), and window_matrix is positive definite.
All inputs are finite; a program needn't handle non-finite values.
Results may differ from the reference program's by a relative error of at most 0.00087.
Values sent between devices are 32-bit elements; how exact they have to be, the bound alone decides.
A program may use at most 128 MiB of HBM per device.

```python
import math
import jax
import jax.numpy as jnp
from jax import lax

GRID = 96
NPHASE = 4096
SEEDS = 512
STEPS = 256
WINDOW = 1024
PRIOR = 26624
FREQS = 4
FIRST_BIN = 64
N_ROW = 4
N_COL = 2


def draw_prior_factor(key, part):
    limit = math.sqrt(0.9) / (math.sqrt(PRIOR) + math.sqrt(WINDOW))
    values = jax.random.uniform(key, (FREQS, PRIOR, WINDOW), jnp.float32, -limit, limit)
    return values.astype(jnp.bfloat16)


def plant(result, stream_key, smallest, high):
    dims = result.shape
    spot = [jax.random.randint(jax.random.fold_in(stream_key, axis), (), 0, dims[axis]) for axis in range(len(dims))]
    result = result.at[tuple(spot)].set(smallest)
    longest = dims.index(max(dims))
    spot[longest] = (spot[longest] + 1) % dims[longest]
    return result.at[tuple(spot)].set(high)


def steps_of(rng, dims, split, least, high):
    def one(axis_at, blocks):
        steps = jax.random.uniform(jax.random.fold_in(jax.random.fold_in(rng, 6), axis_at), (blocks,), jnp.float32, least / len(split), high / len(split))
        return jnp.repeat(jnp.exp(steps), dims[axis_at] // blocks).reshape((-1,) + (1,) * (len(dims) - axis_at - 1))

    gain = one(*split[0])
    for cut in split[1:]:
        gain = gain * one(*cut)
    return gain


def setup_inputs(seed: int = 0) -> dict:
    arg_keys = jax.random.split(jax.random.key(seed), 7)
    return {
        "prior_factor": draw_prior_factor(jax.random.fold_in(arg_keys[6], 71), 0),
        "prior_seeds": plant(jax.random.randint(arg_keys[1], (FREQS, PRIOR, SEEDS), 0, NPHASE), jax.random.fold_in(arg_keys[1], 1), 0, NPHASE - 1).astype(jnp.int32),
        "window_seeds": plant(jax.random.randint(arg_keys[2], (FREQS, WINDOW, SEEDS), 0, NPHASE), jax.random.fold_in(arg_keys[2], 1), 0, NPHASE - 1).astype(jnp.int32),
        "spectra": jnp.clip(jnp.exp(math.log(1.0) - 1.3862944 * jax.random.uniform(arg_keys[3], (FREQS, WINDOW), jnp.float32) ** steps_of(arg_keys[3], (FREQS, WINDOW), ((0, 4),), -0.2, 0.2)), 0.25, 1.0),
        "nugget": jnp.clip(0.6 + 0.6 * jax.random.uniform(arg_keys[4], (FREQS, WINDOW), jnp.float32) ** steps_of(arg_keys[4], (FREQS, WINDOW), ((0, 4),), -0.2, 0.2), 0.6, 1.2),
        "decay": jnp.clip(jnp.exp(math.log(2.0) - 2.3025851 * jax.random.uniform(arg_keys[5], (FREQS,), jnp.float32) ** steps_of(arg_keys[5], (FREQS,), ((0, 4),), -0.2, 0.2)), 0.2, 2.0),
    }


cross_weight = 0.3

def window_index(positions, window, parts):
    own = window // parts
    quarter = own // 2
    device = positions // own
    within = positions % own
    return jnp.where(within < quarter, device * quarter + within, window // 2 + device * quarter + within - quarter).astype(jnp.int32)

def coherence(spectra, nugget, decay, row_ids):
    window = spectra.shape[0]
    col_ids = jnp.arange(window, dtype=jnp.int32)
    row_global = PRIOR + row_ids
    col_global = PRIOR + col_ids
    row_points = row_global // 3
    col_points = col_global // 3
    row_across = (row_points % GRID).astype(jnp.float32)
    row_height = (row_points // GRID).astype(jnp.float32)
    col_across = (col_points % GRID).astype(jnp.float32)
    col_height = (col_points // GRID).astype(jnp.float32)
    distance = jnp.sqrt((row_across[:, None] - col_across[None, :]) ** 2 + (row_height[:, None] - col_height[None, :]) ** 2)
    coupling = jnp.where((row_global % 3)[:, None] == (col_global % 3)[None, :], jnp.float32(1.0), jnp.float32(cross_weight))
    row_spectra = jnp.take(spectra, row_ids)
    row_nugget = jnp.take(nugget, row_ids)
    amplitude = jnp.sqrt(row_spectra[:, None] * spectra[None, :])
    diagonal = jnp.where(row_ids[:, None] == col_ids[None, :], row_nugget[:, None], jnp.float32(0.0))
    return coupling * amplitude * jnp.exp(-decay * distance) + diagonal

def reference(prior_factor, prior_seeds, window_seeds, spectra, nugget, decay):
    re_parts = []
    im_parts = []
    natural_ids = jnp.arange(WINDOW, dtype=jnp.int32)
    for freq_index in range(FREQS):
        prior_cols = prior_factor[freq_index]
        schur = jnp.dot(prior_cols.T.astype(jnp.float32), prior_cols.astype(jnp.float32), preferred_element_type=jnp.float32)
        window_matrix = coherence(spectra[freq_index], nugget[freq_index], decay[freq_index], natural_ids) - schur
        factor = jnp.linalg.cholesky(window_matrix)
        phases = 2.0 * math.pi / NPHASE * prior_seeds[freq_index].astype(jnp.float32)
        wave_re = jnp.cos(phases).astype(jnp.bfloat16)
        wave_im = jnp.sin(phases).astype(jnp.bfloat16)
        prior_re = jnp.dot(prior_cols.T.astype(jnp.float32), wave_re.astype(jnp.float32), preferred_element_type=jnp.float32)
        prior_im = jnp.dot(prior_cols.T.astype(jnp.float32), wave_im.astype(jnp.float32), preferred_element_type=jnp.float32)
        window_phases = 2.0 * math.pi / NPHASE * window_seeds[freq_index].astype(jnp.float32)
        re_parts.append(prior_re + jnp.dot(factor, jnp.cos(window_phases), precision=lax.Precision.HIGHEST))
        im_parts.append(prior_im + jnp.dot(factor, jnp.sin(window_phases), precision=lax.Precision.HIGHEST))
    amp_re = jnp.stack(re_parts)
    amp_im = jnp.stack(im_parts)
    freq_bins = FIRST_BIN + jnp.arange(FREQS, dtype=jnp.int32)
    sample_ids = jnp.arange(STEPS, dtype=jnp.int32)
    turns = (freq_bins[:, None] * sample_ids[None, :] % STEPS).astype(jnp.float32) * (2.0 * math.pi / STEPS)
    first_sum = jnp.einsum('fps,ft->spt', amp_re, jnp.cos(turns), precision=lax.Precision.HIGHEST)
    second_sum = jnp.einsum('fps,ft->spt', amp_im, jnp.sin(turns), precision=lax.Precision.HIGHEST)
    natural = first_sum - second_sum
    stored = window_index(natural_ids, WINDOW, N_ROW * N_COL)
    return jnp.take(natural, stored, axis=1)
```

```python
import functools
import math

import jax
import jax.numpy as jnp
import numpy as np
from jax import lax
from jax.experimental import pallas as pl
from jax.experimental.pallas import tpu as pltpu
from jax.sharding import PartitionSpec as P

GRID = 96
NPHASE = 4096
STEPS = 256
FIRST_BIN = 64
AXES = ("row", "col")
BLOCK = 128
SUB = 8
CROSS_WEIGHT = 0.3

MESH = pl.DeviceIdType.MESH
NT = (((1,), (1,)), ((), ()))
TN = (((0,), (0,)), ((), ()))
NN = (((1,), (0,)), ((), ()))

SIN = (1.5707963200653545, -0.6459637604384879, 0.07968992260046377, -0.004674150668920225, 0.00015167511779068624)
COS = (0.9999999532476089, -1.233698207654912, 0.25365070955391866, -0.020810571376273755, 0.000858162543356229)


def split(x):
    high = x.astype(jnp.bfloat16)
    return high, (x - high.astype(jnp.float32)).astype(jnp.bfloat16)


def dot(a, b, dims):
    return lax.dot_general(a, b, dims, preferred_element_type=jnp.float32)


def mul3(a, b, dims=NT):
    ah, al = a
    bh, bl = b
    return dot(ah, bh, dims) + (dot(ah, bl, dims) + dot(al, bh, dims))


def waves_of(seeds):
    half = NPHASE // 2
    turn = (seeds + half // 2) >> (half.bit_length() - 1)
    z = (seeds - (turn << (half.bit_length() - 1))).astype(jnp.float32) * (2.0 / half)
    y = z * z
    sin, cos = SIN[-1], COS[-1]
    for s in SIN[-2::-1]:
        sin = sin * y + s
    for c in COS[-2::-1]:
        cos = cos * y + c
    sign = jnp.where((turn & 1) == 1, -1.0, 1.0)
    return cos * sign, sin * (z * sign)


def invert_block(m_ref, col_ref, row_ref):
    lane = lax.broadcasted_iota(jnp.int32, (SUB, BLOCK), 1)
    sub = lax.broadcasted_iota(jnp.int32, (SUB, BLOCK), 0)
    strips = BLOCK // SUB
    for p in range(strips):
        j0 = SUB * p
        inside = (lane >= j0) & (lane < j0 + SUB)
        lead = m_ref[j0:j0 + SUB, :]
        for k in range(SUB):
            col_ref[k] = jnp.broadcast_to(lead[:, j0 + k:j0 + k + 1], (SUB, BLOCK))
        row_ref[...] = jnp.where(inside, jnp.where(lane - j0 == sub, 1.0, 0.0), lead)
        a = {}
        for k in range(SUB):
            for i in range(k, SUB):
                a[i, k] = jnp.broadcast_to(col_ref[k, i:i + 1, :], (SUB, BLOCK))
        inv = []
        low = {}
        for k in range(SUB):
            r = lax.rsqrt(a[k, k])
            inv.append(r)
            for i in range(k + 1, SUB):
                low[i, k] = a[i, k] * r
            for m in range(k + 1, SUB):
                for i in range(m, SUB):
                    a[i, m] = a[i, m] - low[i, k] * low[m, k]
        u = []
        for k in range(SUB):
            x = jnp.broadcast_to(row_ref[k:k + 1, :], (SUB, BLOCK))
            for m in range(k):
                x = x - low[k, m] * u[m]
            u.append(x * inv[k])
        w = u[0]
        for k in range(1, SUB):
            w = jnp.where(sub == k, u[k], w)
        m_ref[j0:j0 + SUB, :] = jnp.where(lane < j0 + SUB, w, 0.0)
        for t in range(p + 1, strips):
            at = slice(SUB * t, SUB * t + SUB)
            rows = m_ref[at, :]
            c = []
            for k in range(SUB):
                x = jnp.broadcast_to(rows[:, j0 + k:j0 + k + 1], (SUB, BLOCK))
                for m in range(k):
                    x = x - low[k, m] * c[m]
                c.append(x * inv[k])
            x = jnp.where(inside, 0.0, rows)
            for k in range(SUB):
                x = x - c[k] * u[k]
            m_ref[at, :] = x


def groups_of(window, parts):
    count = window // BLOCK
    lists = [[0], [1], [2, 3], list(range(4, count))] if count > 4 else [[j] for j in range(count)]
    out, at = [], 0
    for panels in lists:
        rows = sum(window - j * BLOCK for j in panels)
        rows = -(-rows // (8 * parts)) * (8 * parts)
        out.append((panels, at, rows))
        at += rows
    return out, at


def farm_kernel(
    parts, n_col, freqs, cols_hbm, seeds_hbm, wseeds_hbm, place_ref, spectra_ref, nugget_ref, decay_ref,
    out_ref, cols_ref, seeds_ref, wseeds_ref, sum_ref, land_ref, prod_ref, pland_ref, dland_ref, coh_ref,
    featr_ref, featc_ref, fin_ref, lh_ref, ll_ref, wh_ref, wl_ref, m_ref, col_ref, row_ref, pan_ref, ih_ref, il_ref,
    send_ref, load_sem, ar_send, ar_recv, ps_send, ps_recv, fs_send, fs_recv,
):
    depth, window = cols_ref.shape
    seed_count = seeds_ref.shape[1]
    quarter = window // (2 * parts)
    here_count = seed_count // freqs
    blocks = window // BLOCK
    chips = parts // 2
    stages = parts.bit_length() - 1
    me = lax.axis_index("row") * n_col + lax.axis_index("col")
    mine_f = lax.axis_index("freq")
    core = me % 2
    chip = me // 2

    quads = 4 if depth % 64 == 0 else 1
    part_rows = depth // quads
    loads = []
    for i in range(quads):
        at = slice(i * part_rows, (i + 1) * part_rows)
        loads.append(pltpu.make_async_copy(cols_hbm.at[at], cols_ref.at[at], load_sem.at[i]))
    seed_load = pltpu.make_async_copy(seeds_hbm, seeds_ref, load_sem.at[quads])
    wseed_load = pltpu.make_async_copy(wseeds_hbm, wseeds_ref, load_sem.at[quads + 1])
    for copy in loads + [seed_load, wseed_load]:
        copy.start()

    def plane(index):
        return {"row": index // n_col, "col": index % n_col}

    def partner(bit):
        return plane(me + bit * (1 - 2 * ((me // bit) % 2)))

    def same_core(shift):
        return plane(2 * ((chip + shift) % chips) + core)

    def along_freq(shift):
        return {"freq": (mine_f + shift) % freqs}

    barrier = pltpu.get_barrier_semaphore()
    meet = [partner(1)] + [same_core(j) for j in range(1, chips)] + [along_freq(j) for j in range(1, freqs)]
    for other in meet:
        pl.semaphore_signal(barrier, inc=1, device_id=other, device_id_type=MESH)

    upper = [2**s for s in range(1, stages)]
    turned = upper[1:] + upper[:1]
    bits = [1] + [a + core * (b - a) for a, b in zip(upper, turned)]

    lists, total_rows = groups_of(window, parts)
    panel_at = {}
    for panels, at, rows in lists:
        for j in panels:
            panel_at[j] = at
            at += window - j * BLOCK

    class Group:
        def __init__(self, index):
            self.index = index
            self.start, self.size = lists[index][1], lists[index][2]
            self.slot = self.start
            self.kept, self.stage, self.copy = [], 0, None

        def launch(self):
            s = self.stage
            if s == 2 * stages:
                self.copy = None
                return
            if s < stages:
                self.size //= 2
                bit = bits[s]
                mine = (me // bit) % 2
                self.keep = pl.ds(pl.multiple_of(self.start + mine * self.size, 8), self.size)
                source = sum_ref.at[pl.ds(pl.multiple_of(self.start + (1 - mine) * self.size, 8), self.size)]
                self.landed = slice(self.slot, self.slot + self.size)
                target = land_ref.at[self.landed]
                self.kept.append(self.keep)
                self.start = self.start + mine * self.size
                self.slot += self.size
            else:
                back = 2 * stages - 1 - s
                bit = bits[back]
                source = target = fin_ref.at[self.kept[back]]
            self.copy = pltpu.make_async_remote_copy(
                src_ref=source, dst_ref=target,
                send_sem=ar_send.at[self.index, s], recv_sem=ar_recv.at[self.index, s],
                device_id=partner(bit), device_id_type=MESH,
            )
            self.copy.start()

        def advance(self):
            if self.copy is None:
                return
            self.copy.wait()
            if self.stage < stages:
                total_ref = fin_ref if self.stage == stages - 1 else sum_ref
                total_ref[self.keep, :] = sum_ref[self.keep, :] + land_ref[self.landed, :]
            self.stage += 1
            self.launch()

    groups = [Group(i) for i in range(len(lists))]
    flying = []

    def advance():
        for group in flying:
            group.advance()

    def wide_panels(pair):
        c0 = pair * 2 * BLOCK
        for r0 in range(c0, window, 2 * BLOCK):
            tile = dot(cols_ref[:, r0:r0 + 2 * BLOCK], cols_ref[:, c0:c0 + 2 * BLOCK], TN)
            a = panel_at[2 * pair] + r0 - c0
            sum_ref[a:a + 2 * BLOCK, :] = tile[:, :BLOCK]
            b = panel_at[2 * pair + 1] + r0 - c0 - BLOCK
            if r0 == c0:
                sum_ref[b + BLOCK:b + 2 * BLOCK, :] = tile[BLOCK:, BLOCK:]
            else:
                sum_ref[b:b + 2 * BLOCK, :] = tile[:, BLOCK:]

    def coherences():
        for i in range(3):
            featr_ref[i:i + 1, :] = place_ref[i:i + 1, :]
        featr_ref[3:4, :] = jnp.sqrt(spectra_ref[...])
        featr_ref[4:5, :] = nugget_ref[...]
        featr_ref[5:6, :] = jnp.broadcast_to(decay_ref[...], (1, window))
        featr_ref[6:8, :] = jnp.zeros((2, window), jnp.float32)
        for t in range(blocks):
            featc_ref[t * BLOCK:(t + 1) * BLOCK, :] = jnp.transpose(featr_ref[:, t * BLOCK:(t + 1) * BLOCK])
        row_id = lax.broadcasted_iota(jnp.int32, (BLOCK, BLOCK), 0)
        col_id = lax.broadcasted_iota(jnp.int32, (BLOCK, BLOCK), 1)

        @pl.loop(0, blocks)
        def _(b):
            at = b * window - (BLOCK // 2) * b * (b - 1)
            across = pl.ds(pl.multiple_of(b * BLOCK, BLOCK), BLOCK)

            def of_col(i):
                return featr_ref[i:i + 1, across]

            @pl.loop(b, blocks)
            def _(t):
                rows = pl.ds(pl.multiple_of(t * BLOCK, BLOCK), BLOCK)

                def of_row(i):
                    return featc_ref[rows, i:i + 1]

                dx = of_row(0) - of_col(0)
                dy = of_row(1) - of_col(1)
                distance = jnp.sqrt(dx * dx + dy * dy)
                weight = jnp.where(of_row(2) == of_col(2), 1.0, CROSS_WEIGHT)
                value = weight * (of_row(3) * of_col(3)) * jnp.exp(-of_col(5) * distance)
                same = (row_id + t * BLOCK) == (col_id + b * BLOCK)
                value = value + jnp.where(same, of_row(4), 0.0)
                there = pl.ds(pl.multiple_of(at + (t - b) * BLOCK, BLOCK), BLOCK)
                coh_ref[there, :] = value

    chunk = next(c for c in (256, 208, 128, 64, 32, 16) if depth % c == 0)
    chunks = depth // chunk
    tall = min(256, window // 2)

    def products(first, last):
        @pl.loop(first, last)
        def _(step):
            at = pl.ds(pl.multiple_of(step * chunk, chunk), chunk)
            wave_re, wave_im = waves_of(seeds_ref[at, :])
            waves = jnp.concatenate([wave_re.astype(jnp.bfloat16), wave_im.astype(jnp.bfloat16)], axis=1)
            for r in range(window // tall):
                term = dot(cols_ref[at, r * tall:(r + 1) * tall], waves, TN)
                term = term.reshape(tall // (2 * quarter), 2, quarter, 2 * seed_count)
                half, base = divmod(r * tall, window // 2)
                there = slice(base // (2 * quarter), (base + tall) // (2 * quarter))
                prod_ref[there, :, half] += term

    def window_waves(first, last):
        @pl.loop(first, last)
        def _(t):
            at = pl.ds(pl.multiple_of(t * BLOCK, BLOCK), BLOCK)
            wave_re, wave_im = waves_of(wseeds_ref[at, :])
            for i, wave in enumerate((wave_re, wave_im)):
                high, low = split(wave)
                wh_ref[at, i * seed_count:(i + 1) * seed_count] = high
                wl_ref[at, i * seed_count:(i + 1) * seed_count] = low

    def core_copy():
        return pltpu.make_async_remote_copy(
            src_ref=prod_ref.at[:, 1 - core], dst_ref=pland_ref,
            send_sem=ps_send.at[0], recv_sem=ps_recv.at[0],
            device_id=partner(1), device_id_type=MESH,
        )

    def chip_copy(j):
        return pltpu.make_async_remote_copy(
            src_ref=prod_ref.at[(chip + j) % chips, core], dst_ref=dland_ref.at[j - 1],
            send_sem=ps_send.at[j], recv_sem=ps_recv.at[j],
            device_id=same_core(j), device_id_type=MESH,
        )

    for copy in loads:
        copy.wait()
    pl.semaphore_wait(barrier, len(meet))
    done = 0
    for pair in range(blocks // 2):
        wide_panels(pair)
        advance()
        while done < len(groups) and max(lists[done][0]) <= 2 * pair + 1:
            groups[done].launch()
            flying.append(groups[done])
            done += 1
    prod_ref[...] = jnp.zeros_like(prod_ref)
    coherences()
    advance()
    seed_load.wait()
    cuts = [chunks * i // 5 for i in range(6)]
    for i in range(5):
        products(cuts[i], cuts[i + 1])
        if i == 4:
            to_sibling = core_copy()
            to_sibling.start()
        advance()
    wseed_load.wait()
    window_waves(0, blocks // 2)
    advance()
    to_sibling.wait()

    @pl.loop(0, chips)
    def _(i):
        prod_ref[i, core] = prod_ref[i, core] + pland_ref[i]

    chip_copies = [chip_copy(j) for j in range(1, chips)]
    for copy in chip_copies:
        copy.start()
    window_waves(blocks // 2, blocks)
    while any(group.copy is not None for group in flying):
        advance()

    def matrix(b, first, last):
        at = panel_at[b] + first - b * BLOCK
        mark = b * window - (BLOCK // 2) * b * (b - 1) + first - b * BLOCK
        return coh_ref[mark:mark + last - first, :] - fin_ref[at:at + last - first, :]

    lower = lax.broadcasted_iota(jnp.int32, (BLOCK, BLOCK), 0) >= lax.broadcasted_iota(jnp.int32, (BLOCK, BLOCK), 1)
    lh_ref[...] = jnp.zeros_like(lh_ref)
    ll_ref[...] = jnp.zeros_like(ll_ref)
    m_ref[...] = matrix(0, 0, BLOCK)
    diag = m_ref[...]
    for b in range(blocks):
        at = b * BLOCK
        hi = at + BLOCK
        here = slice(at, hi)
        if 0 < b < blocks - 1:
            ph, pl_ = split(mul3(split(pan_ref[hi:, :]), (ih_ref[...], il_ref[...])))
            lh_ref[hi:, at - BLOCK:at] = ph
            ll_ref[hi:, at - BLOCK:at] = pl_
        if b < blocks - 1:
            nxt = slice(hi, hi + BLOCK)
            pan = matrix(b, hi, window)
            dn = matrix(b + 1, hi, hi + BLOCK)
            if b > 0:
                pan = pan - mul3((lh_ref[hi:, :at], ll_ref[hi:, :at]), (lh_ref[here, :at], ll_ref[here, :at]))
                near = (lh_ref[nxt, :at], ll_ref[nxt, :at])
                dn = dn - mul3(near, near)
            pan_ref[hi:, :] = pan
        invert_block(m_ref, col_ref, row_ref)
        inverse = split(m_ref[...])
        lb = split(jnp.where(lower, mul3(split(diag), inverse), 0.0))
        lh_ref[here, here], ll_ref[here, here] = lb
        if b < blocks - 1:
            ih_ref[...], il_ref[...] = inverse
            near = split(mul3(split(pan_ref[nxt, :]), inverse))
            lh_ref[nxt, here], ll_ref[nxt, here] = near
            diag = dn - mul3(near, near)
            m_ref[...] = diag

    for copy in chip_copies:
        copy.wait()
    prior = prod_ref[chip, core]
    for j in range(1, chips):
        prior = prior + dland_ref[j - 1]
    for half in range(2):
        at = pl.ds(pl.multiple_of(half * (window // 2) + me * quarter, quarter), quarter)
        amp = prior[half] + mul3((lh_ref[at, :], ll_ref[at, :]), (wh_ref[...], wl_ref[...]), NN)
        for i in range(2 * seed_count // BLOCK):
            s0 = i * BLOCK % seed_count
            send_ref[i * BLOCK // seed_count, s0:s0 + BLOCK, half * quarter:(half + 1) * quarter] = jnp.transpose(
                amp[:, i * BLOCK:(i + 1) * BLOCK]
            )

    def seeds_for(f):
        return send_ref.at[:, pl.ds(pl.multiple_of(f * here_count, 8), here_count), :]

    spread = []
    for j in range(1, freqs):
        spread.append(pltpu.make_async_remote_copy(
            src_ref=seeds_for((mine_f + j) % freqs), dst_ref=out_ref.at[pl.ds(2 * mine_f, 2)],
            send_sem=fs_send.at[j - 1], recv_sem=fs_recv.at[j - 1],
            device_id=along_freq(j), device_id_type=MESH,
        ))
    for copy in spread:
        copy.start()
    out_ref[pl.ds(2 * mine_f, 2)] = send_ref[:, pl.ds(pl.multiple_of(mine_f * here_count, 8), here_count), :]
    for copy in spread:
        copy.wait()


def farm(cols, seeds, wseeds, place, spectra, nugget, decay, parts, n_col, freqs):
    depth, window = cols.shape
    seed_count = seeds.shape[1]
    quarter = window // (2 * parts)
    chips = parts // 2
    stages = parts.bit_length() - 1
    lists, total_rows = groups_of(window, parts)
    f32, bf16 = jnp.float32, jnp.bfloat16
    return pl.pallas_call(
        functools.partial(farm_kernel, parts, n_col, freqs),
        name="farm",
        out_shape=jax.ShapeDtypeStruct((2 * freqs, seed_count // freqs, 2 * quarter), f32),
        in_specs=[pl.BlockSpec(memory_space=pl.ANY)] * 3 + [pl.BlockSpec(memory_space=pltpu.VMEM)] * 4,
        out_specs=pl.BlockSpec(memory_space=pltpu.VMEM),
        scratch_shapes=[
            pltpu.VMEM(cols.shape, bf16),
            pltpu.VMEM(seeds.shape, jnp.int32),
            pltpu.VMEM(wseeds.shape, jnp.int32),
            pltpu.VMEM((total_rows, BLOCK), f32),
            pltpu.VMEM((total_rows, BLOCK), f32),
            pltpu.VMEM((chips, 2, 2, quarter, 2 * seed_count), f32),
            pltpu.VMEM((chips, 2, quarter, 2 * seed_count), f32),
            pltpu.VMEM((max(chips - 1, 1), 2, quarter, 2 * seed_count), f32),
            pltpu.VMEM((window * (window // BLOCK + 1) // 2, BLOCK), f32),
            pltpu.VMEM((8, window), f32),
            pltpu.VMEM((window, 8), f32),
            pltpu.VMEM((total_rows, BLOCK), f32),
            pltpu.VMEM((window, window), bf16),
            pltpu.VMEM((window, window), bf16),
            pltpu.VMEM((window, 2 * seed_count), bf16),
            pltpu.VMEM((window, 2 * seed_count), bf16),
            pltpu.VMEM((BLOCK, BLOCK), f32),
            pltpu.VMEM((SUB, SUB, BLOCK), f32),
            pltpu.VMEM((SUB, BLOCK), f32),
            pltpu.VMEM((window, BLOCK), f32),
            pltpu.VMEM((BLOCK, BLOCK), bf16),
            pltpu.VMEM((BLOCK, BLOCK), bf16),
            pltpu.VMEM((2, seed_count, 2 * quarter), f32),
            pltpu.SemaphoreType.DMA((6,)),
            pltpu.SemaphoreType.DMA((len(lists), 2 * stages)),
            pltpu.SemaphoreType.DMA((len(lists), 2 * stages)),
            pltpu.SemaphoreType.DMA((chips,)),
            pltpu.SemaphoreType.DMA((chips,)),
            pltpu.SemaphoreType.DMA((freqs,)),
            pltpu.SemaphoreType.DMA((freqs,)),
        ],
        compiler_params=pltpu.CompilerParams(
            collective_id=0, has_side_effects=True, vmem_limit_bytes=60 * 2**20
        ),
    )(cols, seeds, wseeds, place, spectra, nugget, decay)


def synth_kernel(x_ref, table_ref, out_ref):
    def parts(value):
        high = value.astype(jnp.bfloat16).astype(jnp.float32)
        return high, value - high

    xh, xl = parts(x_ref[...])
    th, tl = parts(table_ref[...])
    lhs = jnp.concatenate([xh, xh, xl, xl], axis=0).astype(jnp.bfloat16)
    rhs = jnp.concatenate([th, tl, th, tl], axis=0).astype(jnp.bfloat16)
    out_ref[...] = dot(lhs, rhs, TN)


def synthesize(stacked, freq_count):
    turns = np.arange(FIRST_BIN, FIRST_BIN + freq_count)[:, None] * np.arange(STEPS)[None, :] % STEPS
    angles = turns.astype(np.float64) * (2.0 * math.pi / STEPS)
    tables = np.stack([np.cos(angles), -np.sin(angles)], axis=1).reshape(2 * freq_count, STEPS)
    tables = jnp.asarray(tables.astype(np.float32))
    count = stacked.shape[1]
    step = min(2048, count)
    return pl.pallas_call(
        synth_kernel,
        name="synth",
        grid=(count // step,),
        out_shape=jax.ShapeDtypeStruct((count, STEPS), jnp.float32),
        in_specs=[
            pl.BlockSpec((2 * freq_count, step), lambda i: (0, i)),
            pl.BlockSpec((2 * freq_count, STEPS), lambda i: (0, 0)),
        ],
        out_specs=pl.BlockSpec((step, STEPS), lambda i: (i, 0)),
        compiler_params=pltpu.CompilerParams(vmem_limit_bytes=24 * 2**20),
    )(stacked, tables)


def places(prior, window):
    rows = prior + np.arange(window)
    points = rows // 3
    table = np.zeros((8, window), np.float32)
    table[0], table[1], table[2] = points % GRID, points // GRID, rows % 3
    return jnp.asarray(table)


def shards(prior_factor, prior_seeds, window_seeds, spectra, nugget, decay):
    cols = prior_factor[0]
    depth, window = cols.shape
    parts = lax.axis_size(AXES)
    freq_count = lax.axis_size("freq")
    spread = farm(
        cols, prior_seeds[0], window_seeds[0], places(depth * parts, window), spectra, nugget,
        decay.reshape(1, 1), parts, lax.axis_size("col"), freq_count,
    )
    lines, here, own = spread.shape
    out = synthesize(spread.reshape(lines, here * own), freq_count)
    return out.reshape(here, own, STEPS)


def solution(mesh):
    in_specs = (
        P("freq", ("row", "col"), None),
        P("freq", ("row", "col"), None),
        P("freq", None, None),
        P("freq", None),
        P("freq", None),
        P("freq"),
    )
    out_specs = P("freq", ("row", "col"), None)
    return jax.shard_map(shards, mesh=mesh, in_specs=in_specs, out_specs=out_specs, check_vma=False)
```

```python
import functools

import jax
import jax.numpy as jnp
import numpy as np
from jax import lax
from jax.experimental import pallas as pl
from jax.experimental.pallas import tpu as pltpu
from jax.sharding import PartitionSpec as P

GRID = 96
NPHASE = 4096
STEPS = 256
FIRST_BIN = 64
AXES = ("row", "col")
BLOCK = 128
SUB = 8
CROSS_WEIGHT = 0.3
SYNTH_STEP = 8

MESH = pl.DeviceIdType.MESH
NT = (((1,), (1,)), ((), ()))
TN = (((0,), (0,)), ((), ()))
NN = (((1,), (0,)), ((), ()))

SIN = (1.5707963200653545, -0.6459637604384879, 0.07968992260046377, -0.004674150668920225, 0.00015167511779068624)
COS = (0.9999999532476089, -1.233698207654912, 0.25365070955391866, -0.020810571376273755, 0.000858162543356229)


def split(x):
    high = x.astype(jnp.bfloat16)
    return high, (x - high.astype(jnp.float32)).astype(jnp.bfloat16)


def dot(a, b, dims):
    return lax.dot_general(a, b, dims, preferred_element_type=jnp.float32)


def mul3(a, b, dims=NT):
    ah, al = a
    bh, bl = b
    return dot(ah, bh, dims) + (dot(ah, bl, dims) + dot(al, bh, dims))


def waves_of(seeds):
    half = NPHASE // 2
    turn = (seeds + half // 2) >> (half.bit_length() - 1)
    z = (seeds - (turn << (half.bit_length() - 1))).astype(jnp.float32) * (2.0 / half)
    y = z * z
    sin, cos = SIN[-1], COS[-1]
    for s in SIN[-2::-1]:
        sin = sin * y + s
    for c in COS[-2::-1]:
        cos = cos * y + c
    sign = jnp.where((turn & 1) == 1, -1.0, 1.0)
    return cos * sign, sin * (z * sign)


def invert_block(m_ref, col_ref, row_ref):
    lane = lax.broadcasted_iota(jnp.int32, (SUB, BLOCK), 1)
    sub = lax.broadcasted_iota(jnp.int32, (SUB, BLOCK), 0)
    strips = BLOCK // SUB
    for p in range(strips):
        j0 = SUB * p
        inside = (lane >= j0) & (lane < j0 + SUB)
        lead = m_ref[j0:j0 + SUB, :]
        for k in range(SUB):
            col_ref[k] = jnp.broadcast_to(lead[:, j0 + k:j0 + k + 1], (SUB, BLOCK))
        row_ref[...] = jnp.where(inside, jnp.where(lane - j0 == sub, 1.0, 0.0), lead)
        a = {}
        for k in range(SUB):
            for i in range(k, SUB):
                a[i, k] = jnp.broadcast_to(col_ref[k, i:i + 1, :], (SUB, BLOCK))
        inv = []
        low = {}
        for k in range(SUB):
            r = lax.rsqrt(a[k, k])
            inv.append(r)
            for i in range(k + 1, SUB):
                low[i, k] = a[i, k] * r
            for m in range(k + 1, SUB):
                for i in range(m, SUB):
                    a[i, m] = a[i, m] - low[i, k] * low[m, k]
        u = []
        for k in range(SUB):
            x = jnp.broadcast_to(row_ref[k:k + 1, :], (SUB, BLOCK))
            for m in range(k):
                x = x - low[k, m] * u[m]
            u.append(x * inv[k])
        w = u[0]
        for k in range(1, SUB):
            w = jnp.where(sub == k, u[k], w)
        m_ref[j0:j0 + SUB, :] = jnp.where(lane < j0 + SUB, w, 0.0)
        for t in range(p + 1, strips):
            at = slice(SUB * t, SUB * t + SUB)
            rows = m_ref[at, :]
            c = []
            for k in range(SUB):
                x = jnp.broadcast_to(rows[:, j0 + k:j0 + k + 1], (SUB, BLOCK))
                for m in range(k):
                    x = x - low[k, m] * c[m]
                c.append(x * inv[k])
            x = jnp.where(inside, 0.0, rows)
            for k in range(SUB):
                x = x - c[k] * u[k]
            m_ref[at, :] = x


def groups_of(window, parts):
    count = window // BLOCK
    lists = [[0], [1], [2, 3], list(range(4, count))] if count > 4 else [[j] for j in range(count)]
    out, at = [], 0
    for panels in lists:
        rows = sum(window - j * BLOCK for j in panels)
        rows = -(-rows // (8 * parts)) * (8 * parts)
        out.append((panels, at, rows))
        at += rows
    return out, at


def farm_kernel(
    parts, n_col, freqs, cols_hbm, seeds_hbm, wseeds_hbm, place_ref, spectra_ref, nugget_ref, decay_ref,
    out_ref, cols_ref, seeds_ref, wseeds_ref, sum_ref, land_ref, prod_ref, pland_ref, dland_ref, coh_ref,
    featr_ref, featc_ref, fin_ref, lh_ref, ll_ref, wh_ref, wl_ref, m_ref, col_ref, row_ref, pan_ref, ih_ref, il_ref,
    acc_ref, tr_ref, send_ref, load_sem, ar_send, ar_recv, ps_send, ps_recv, fs_send, fs_recv,
):
    depth, window = cols_ref.shape
    seed_count = seeds_ref.shape[1]
    quarter = window // (2 * parts)
    pair_count = seed_count // freqs // 2
    blocks = window // BLOCK
    chips = parts // 2
    stages = parts.bit_length() - 1
    me = lax.axis_index("row") * n_col + lax.axis_index("col")
    mine_f = lax.axis_index("freq")
    core = me % 2
    chip = me // 2

    quads = 4 if depth % 64 == 0 else 1
    part_rows = depth // quads
    loads = []
    for i in range(quads):
        at = slice(i * part_rows, (i + 1) * part_rows)
        loads.append(pltpu.make_async_copy(cols_hbm.at[at], cols_ref.at[at], load_sem.at[i]))
    seed_load = pltpu.make_async_copy(seeds_hbm, seeds_ref, load_sem.at[quads])
    wseed_load = pltpu.make_async_copy(wseeds_hbm, wseeds_ref, load_sem.at[quads + 1])
    for copy in loads + [seed_load, wseed_load]:
        copy.start()

    def plane(index):
        return {"row": index // n_col, "col": index % n_col}

    def partner(bit):
        return plane(me + bit * (1 - 2 * ((me // bit) % 2)))

    def same_core(shift):
        return plane(2 * ((chip + shift) % chips) + core)

    def along_freq(shift):
        return {"freq": (mine_f + shift) % freqs}

    barrier = pltpu.get_barrier_semaphore()
    meet = [partner(1)] + [same_core(j) for j in range(1, chips)] + [along_freq(j) for j in range(1, freqs)]
    for other in meet:
        pl.semaphore_signal(barrier, inc=1, device_id=other, device_id_type=MESH)

    upper = [2**s for s in range(1, stages)]
    turned = upper[1:] + upper[:1]
    bits = [1] + [a + core * (b - a) for a, b in zip(upper, turned)]

    lists, total_rows = groups_of(window, parts)
    panel_at = {}
    for panels, at, rows in lists:
        for j in panels:
            panel_at[j] = at
            at += window - j * BLOCK

    class Group:
        def __init__(self, index):
            self.index = index
            self.start, self.size = lists[index][1], lists[index][2]
            self.slot = self.start
            self.kept, self.stage, self.copy = [], 0, None

        def launch(self):
            s = self.stage
            if s == 2 * stages:
                self.copy = None
                return
            if s < stages:
                self.size //= 2
                bit = bits[s]
                mine = (me // bit) % 2
                self.keep = pl.ds(pl.multiple_of(self.start + mine * self.size, 8), self.size)
                source = sum_ref.at[pl.ds(pl.multiple_of(self.start + (1 - mine) * self.size, 8), self.size)]
                self.landed = slice(self.slot, self.slot + self.size)
                target = land_ref.at[self.landed]
                self.kept.append(self.keep)
                self.start = self.start + mine * self.size
                self.slot += self.size
            else:
                back = 2 * stages - 1 - s
                bit = bits[back]
                source = target = fin_ref.at[self.kept[back]]
            self.copy = pltpu.make_async_remote_copy(
                src_ref=source, dst_ref=target,
                send_sem=ar_send.at[self.index, s], recv_sem=ar_recv.at[self.index, s],
                device_id=partner(bit), device_id_type=MESH,
            )
            self.copy.start()

        def advance(self):
            if self.copy is None:
                return
            self.copy.wait()
            if self.stage < stages:
                total_ref = fin_ref if self.stage == stages - 1 else sum_ref
                total_ref[self.keep, :] = sum_ref[self.keep, :] + land_ref[self.landed, :]
            self.stage += 1
            self.launch()

    groups = [Group(i) for i in range(len(lists))]
    group_of = {j: groups[i] for i, entry in enumerate(lists) for j in entry[0]}

    def advance(*which):
        for i in which:
            if i < len(groups):
                groups[i].advance()

    def require(panel):
        while group_of[panel].copy is not None:
            group_of[panel].advance()

    def wide_panels(pair):
        c0 = pair * 2 * BLOCK
        for r0 in range(c0, window, 2 * BLOCK):
            tile = dot(cols_ref[:, r0:r0 + 2 * BLOCK], cols_ref[:, c0:c0 + 2 * BLOCK], TN)
            a = panel_at[2 * pair] + r0 - c0
            sum_ref[a:a + 2 * BLOCK, :] = tile[:, :BLOCK]
            b = panel_at[2 * pair + 1] + r0 - c0 - BLOCK
            if r0 == c0:
                sum_ref[b + BLOCK:b + 2 * BLOCK, :] = tile[BLOCK:, BLOCK:]
            else:
                sum_ref[b:b + 2 * BLOCK, :] = tile[:, BLOCK:]

    def coherences():
        for i in range(3):
            featr_ref[i:i + 1, :] = place_ref[i:i + 1, :]
        featr_ref[3:4, :] = jnp.sqrt(spectra_ref[...])
        featr_ref[4:5, :] = nugget_ref[...]
        featr_ref[5:6, :] = jnp.broadcast_to(decay_ref[...], (1, window))
        featr_ref[6:8, :] = jnp.zeros((2, window), jnp.float32)
        for t in range(blocks):
            featc_ref[t * BLOCK:(t + 1) * BLOCK, :] = jnp.transpose(featr_ref[:, t * BLOCK:(t + 1) * BLOCK])
        row_id = lax.broadcasted_iota(jnp.int32, (BLOCK, BLOCK), 0)
        col_id = lax.broadcasted_iota(jnp.int32, (BLOCK, BLOCK), 1)

        @pl.loop(0, blocks)
        def _(b):
            at = b * window - (BLOCK // 2) * b * (b - 1)
            across = pl.ds(pl.multiple_of(b * BLOCK, BLOCK), BLOCK)

            def of_col(i):
                return featr_ref[i:i + 1, across]

            @pl.loop(b, blocks)
            def _(t):
                rows = pl.ds(pl.multiple_of(t * BLOCK, BLOCK), BLOCK)

                def of_row(i):
                    return featc_ref[rows, i:i + 1]

                dx = of_row(0) - of_col(0)
                dy = of_row(1) - of_col(1)
                distance = jnp.sqrt(dx * dx + dy * dy)
                weight = jnp.where(of_row(2) == of_col(2), 1.0, CROSS_WEIGHT)
                value = weight * (of_row(3) * of_col(3)) * jnp.exp(-of_col(5) * distance)
                same = (row_id + t * BLOCK) == (col_id + b * BLOCK)
                value = value + jnp.where(same, of_row(4), 0.0)
                there = pl.ds(pl.multiple_of(at + (t - b) * BLOCK, BLOCK), BLOCK)
                coh_ref[there, :] = value

    chunk = next(c for c in (256, 208, 128, 64, 32, 16) if depth % c == 0)
    chunks = depth // chunk
    tall = min(256, window // 2)

    def products(first, last):
        @pl.loop(first, last)
        def _(step):
            at = pl.ds(pl.multiple_of(step * chunk, chunk), chunk)
            wave_re, wave_im = waves_of(seeds_ref[at, :])
            waves = jnp.concatenate([wave_re.astype(jnp.bfloat16), wave_im.astype(jnp.bfloat16)], axis=1)
            for r in range(window // tall):
                term = dot(cols_ref[at, r * tall:(r + 1) * tall], waves, TN)
                term = term.reshape(tall // (2 * quarter), 2, quarter, 2 * seed_count)
                half, base = divmod(r * tall, window // 2)
                there = slice(base // (2 * quarter), (base + tall) // (2 * quarter))
                prod_ref[there, :, half] += term

    def window_waves(first, last):
        @pl.loop(first, last)
        def _(t):
            at = pl.ds(pl.multiple_of(t * BLOCK, BLOCK), BLOCK)
            wave_re, wave_im = waves_of(wseeds_ref[at, :])
            for i, wave in enumerate((wave_re, wave_im)):
                high, low = split(wave)
                wh_ref[at, i * seed_count:(i + 1) * seed_count] = high
                wl_ref[at, i * seed_count:(i + 1) * seed_count] = low

    to_sibling = pltpu.make_async_remote_copy(
        src_ref=prod_ref.at[:, 1 - core], dst_ref=pland_ref,
        send_sem=ps_send.at[0, 0], recv_sem=ps_recv.at[0, 0],
        device_id=partner(1), device_id_type=MESH,
    )

    def chip_copy(half, j):
        return pltpu.make_async_remote_copy(
            src_ref=prod_ref.at[(chip + j) % chips, core, half], dst_ref=dland_ref.at[j - 1, half],
            send_sem=ps_send.at[half, j], recv_sem=ps_recv.at[half, j],
            device_id=same_core(j), device_id_type=MESH,
        )

    chip_copies = [[chip_copy(half, j) for j in range(1, chips)] for half in range(2)]

    def spread_prior(half):
        @pl.loop(0, chips)
        def _(i):
            prod_ref[i, core, half] = prod_ref[i, core, half] + pland_ref[i, half]

        for copy in chip_copies[half]:
            copy.start()

    def prior_sum(half):
        for copy in chip_copies[half]:
            copy.wait()
        total = prod_ref[chip, core, half]
        for j in range(1, chips):
            total = total + dland_ref[j - 1, half]
        return total

    def own_rows(half, first, last):
        at = pl.ds(pl.multiple_of(half * (window // 2) + me * quarter, quarter), quarter)
        factor = (lh_ref[at, first:last], ll_ref[at, first:last])
        return mul3(factor, (wh_ref[first:last, :], wl_ref[first:last, :]), NN)

    def freq_copy(half, j):
        other = (mine_f + j) % freqs
        return pltpu.make_async_remote_copy(
            src_ref=send_ref.at[half, :, pl.ds(pl.multiple_of(other * pair_count, 8), pair_count), :],
            dst_ref=out_ref.at[half, pl.ds(2 * mine_f, 2)],
            send_sem=fs_send.at[half, j], recv_sem=fs_recv.at[half, j],
            device_id=along_freq(j), device_id_type=MESH,
        )

    freq_copies = [[freq_copy(half, j) for j in range(1, freqs)] for half in range(2)]

    def send_rows(half, amp):
        for i in range(2 * seed_count // BLOCK):
            tr_ref[i * BLOCK:(i + 1) * BLOCK, :] = jnp.transpose(amp[:, i * BLOCK:(i + 1) * BLOCK])
        for i in range(2 * freqs):
            part, f = divmod(i, freqs)
            there = slice(f * pair_count, (f + 1) * pair_count)
            for side in range(2):
                base = (2 * i + side) * pair_count
                lanes = slice(side * quarter, (side + 1) * quarter)
                send_ref[half, part, there, lanes] = tr_ref[base:base + pair_count, :]
        for copy in freq_copies[half]:
            copy.start()
        own = pl.ds(pl.multiple_of(mine_f * pair_count, 8), pair_count)
        out_ref[half, pl.ds(2 * mine_f, 2)] = send_ref[half, :, own, :]

    for copy in loads:
        copy.wait()
    pl.semaphore_wait(barrier, len(meet))
    def launch(*which):
        for i in which:
            if i < len(groups):
                groups[i].launch()

    for pair in range(blocks // 2):
        wide_panels(pair)
        if pair == 0:
            launch(0, 1)
        elif pair <= 2:
            advance(pair - 1)
        if pair == 2:
            launch(2)
    prod_ref[...] = jnp.zeros_like(prod_ref)
    lh_ref[...] = jnp.zeros_like(lh_ref)
    ll_ref[...] = jnp.zeros_like(ll_ref)
    seed_load.wait()
    launches = {2: (3,)}
    polls = {
        0: (0,), 1: (1, 2), 3: (0,), 4: (1, 3), 5: (2,), 6: (0,), 7: (1,), 8: (3, 2), 10: (0,), 11: (1, 3), 12: (2, 0),
    }
    for i in range(13):
        if chunks * i // 13 < chunks * (i + 1) // 13:
            products(chunks * i // 13, chunks * (i + 1) // 13)
        launch(*launches.get(i, ()))
        advance(*polls.get(i, ()))
    coherences()
    advance(1, 3)
    wseed_load.wait()
    window_waves(0, blocks // 2)
    advance(2)
    window_waves(blocks // 2, blocks)
    advance(3, 2)
    to_sibling.start()
    require(0)

    def matrix(b, first, last):
        at = panel_at[b] + first - b * BLOCK
        mark = b * window - (BLOCK // 2) * b * (b - 1) + first - b * BLOCK
        return coh_ref[mark:mark + last - first, :] - fin_ref[at:at + last - first, :]

    lower = lax.broadcasted_iota(jnp.int32, (BLOCK, BLOCK), 0) >= lax.broadcasted_iota(jnp.int32, (BLOCK, BLOCK), 1)
    m_ref[...] = matrix(0, 0, BLOCK)
    diag = m_ref[...]
    early = max(blocks - 2, blocks // 2)
    for b in range(blocks):
        at = b * BLOCK
        hi = at + BLOCK
        here = slice(at, hi)
        if b < blocks - 1:
            require(b + 1)
        if b == min(1, blocks - 1):
            for j in range(blocks):
                require(j)
            to_sibling.wait()
            spread_prior(0)
            spread_prior(1)
        if 0 < b < blocks - 1:
            ph, pl_ = split(mul3(split(pan_ref[hi:, :]), (ih_ref[...], il_ref[...])))
            lh_ref[hi:, at - BLOCK:at] = ph
            ll_ref[hi:, at - BLOCK:at] = pl_
        if b < blocks - 1:
            nxt = slice(hi, hi + BLOCK)
            pan = matrix(b, hi, window)
            dn = matrix(b + 1, hi, hi + BLOCK)
            if b > 0:
                pan = pan - mul3((lh_ref[hi:, :at], ll_ref[hi:, :at]), (lh_ref[here, :at], ll_ref[here, :at]))
                near = (lh_ref[nxt, :at], ll_ref[nxt, :at])
                dn = dn - mul3(near, near)
            pan_ref[hi:, :] = pan
        if b == early:
            send_rows(0, prior_sum(0) + own_rows(0, 0, window // 2))
        if b == blocks - 1:
            acc_ref[...] = own_rows(1, 0, at)
        invert_block(m_ref, col_ref, row_ref)
        inverse = split(m_ref[...])
        lb = split(jnp.where(lower, mul3(split(diag), inverse), 0.0))
        lh_ref[here, here], ll_ref[here, here] = lb
        if b < blocks - 1:
            ih_ref[...], il_ref[...] = inverse
            near = split(mul3(split(pan_ref[nxt, :]), inverse))
            lh_ref[nxt, here], ll_ref[nxt, here] = near
            diag = dn - mul3(near, near)
            m_ref[...] = diag

    send_rows(1, acc_ref[...] + own_rows(1, window - BLOCK, window) + prior_sum(1))
    for copy in freq_copies[0] + freq_copies[1]:
        copy.wait()


def farm(cols, seeds, wseeds, place, spectra, nugget, decay, parts, n_col, freqs):
    depth, window = cols.shape
    seed_count = seeds.shape[1]
    quarter = window // (2 * parts)
    chips = parts // 2
    stages = parts.bit_length() - 1
    lists, total_rows = groups_of(window, parts)
    f32, bf16 = jnp.float32, jnp.bfloat16
    return pl.pallas_call(
        functools.partial(farm_kernel, parts, n_col, freqs),
        name="farm",
        out_shape=jax.ShapeDtypeStruct((2, 2 * freqs, seed_count // freqs // 2, 2 * quarter), f32),
        in_specs=[pl.BlockSpec(memory_space=pl.ANY)] * 3 + [pl.BlockSpec(memory_space=pltpu.VMEM)] * 4,
        out_specs=pl.BlockSpec(memory_space=pltpu.VMEM),
        scratch_shapes=[
            pltpu.VMEM(cols.shape, bf16),
            pltpu.VMEM(seeds.shape, jnp.int32),
            pltpu.VMEM(wseeds.shape, jnp.int32),
            pltpu.VMEM((total_rows, BLOCK), f32),
            pltpu.VMEM((total_rows, BLOCK), f32),
            pltpu.VMEM((chips, 2, 2, quarter, 2 * seed_count), f32),
            pltpu.VMEM((chips, 2, quarter, 2 * seed_count), f32),
            pltpu.VMEM((max(chips - 1, 1), 2, quarter, 2 * seed_count), f32),
            pltpu.VMEM((window * (window // BLOCK + 1) // 2, BLOCK), f32),
            pltpu.VMEM((8, window), f32),
            pltpu.VMEM((window, 8), f32),
            pltpu.VMEM((total_rows, BLOCK), f32),
            pltpu.VMEM((window, window), bf16),
            pltpu.VMEM((window, window), bf16),
            pltpu.VMEM((window, 2 * seed_count), bf16),
            pltpu.VMEM((window, 2 * seed_count), bf16),
            pltpu.VMEM((BLOCK, BLOCK), f32),
            pltpu.VMEM((SUB, SUB, BLOCK), f32),
            pltpu.VMEM((SUB, BLOCK), f32),
            pltpu.VMEM((window, BLOCK), f32),
            pltpu.VMEM((BLOCK, BLOCK), bf16),
            pltpu.VMEM((BLOCK, BLOCK), bf16),
            pltpu.VMEM((quarter, 2 * seed_count), f32),
            pltpu.VMEM((2 * seed_count, quarter), f32),
            pltpu.VMEM((2, 2, seed_count // 2, 2 * quarter), f32),
            pltpu.SemaphoreType.DMA((6,)),
            pltpu.SemaphoreType.DMA((len(lists), 2 * stages)),
            pltpu.SemaphoreType.DMA((len(lists), 2 * stages)),
            pltpu.SemaphoreType.DMA((2, chips)),
            pltpu.SemaphoreType.DMA((2, chips)),
            pltpu.SemaphoreType.DMA((2, freqs)),
            pltpu.SemaphoreType.DMA((2, freqs)),
        ],
        compiler_params=pltpu.CompilerParams(
            collective_id=0, has_side_effects=True, vmem_limit_bytes=60 * 2**20
        ),
    )(cols, seeds, wseeds, place, spectra, nugget, decay)


def synth_kernel(step, x_ref, out_hbm, buf_ref, sem):
    def parts(value):
        high = value.astype(jnp.bfloat16).astype(jnp.float32)
        return high, value - high

    line = lax.broadcasted_iota(jnp.int32, (x_ref.shape[1], STEPS), 0)
    sample = lax.broadcasted_iota(jnp.int32, (x_ref.shape[1], STEPS), 1)
    turns = ((FIRST_BIN + (line >> 1)) * sample) & (STEPS - 1)
    cos, sin = waves_of(turns * (NPHASE // STEPS))
    th, tl = parts(jnp.where((line & 1) == 0, cos, -sin))
    rhs = jnp.concatenate([th, tl, th, tl], axis=0).astype(jnp.bfloat16)
    pairs = x_ref.shape[2]
    steps = pairs // step

    def copies(c):
        half, first = c // steps, pl.multiple_of(c % steps * step, 8)
        return [
            pltpu.make_async_copy(
                buf_ref.at[c, side], out_hbm.at[side, pl.ds(first, step), half], sem.at[c, side]
            )
            for side in range(2)
        ]

    @pl.loop(0, 2 * steps)
    def _(c):
        half, first = c // steps, pl.multiple_of(c % steps * step, 8)
        xh, xl = parts(jnp.transpose(x_ref[half, :, pl.ds(first, step), :], (1, 0, 2)))
        lhs = jnp.concatenate([xh, xh, xl, xl], axis=1).astype(jnp.bfloat16)
        for i in range(step):
            series = dot(lhs[i], rhs, TN)
            buf_ref[c, :, i] = series.reshape(2, buf_ref.shape[3], buf_ref.shape[4])
        for copy in copies(c):
            copy.start()

    @pl.loop(0, 2 * steps)
    def _(c):
        for copy in copies(c):
            copy.wait()


def synthesize(spread):
    _, lines, pairs, wide = spread.shape
    quarter = wide // 2
    step = min(SYNTH_STEP, pairs)
    chunks = 2 * pairs // step
    return pl.pallas_call(
        functools.partial(synth_kernel, step),
        name="synth",
        out_shape=jax.ShapeDtypeStruct((2, pairs, 2, quarter, STEPS), jnp.float32),
        in_specs=[pl.BlockSpec(memory_space=pltpu.VMEM)],
        out_specs=pl.BlockSpec(memory_space=pl.ANY),
        scratch_shapes=[
            pltpu.VMEM((chunks, 2, step, quarter, STEPS), jnp.float32),
            pltpu.SemaphoreType.DMA((chunks, 2)),
        ],
        compiler_params=pltpu.CompilerParams(vmem_limit_bytes=32 * 2**20),
    )(spread)


def places(prior, window):
    rows = prior + np.arange(window)
    points = rows // 3
    table = np.zeros((8, window), np.float32)
    table[0], table[1], table[2] = points % GRID, points // GRID, rows % 3
    return jnp.asarray(table)


def shards(prior_factor, prior_seeds, window_seeds, spectra, nugget, decay):
    cols = prior_factor[0]
    depth, window = cols.shape
    parts = lax.axis_size(AXES)
    freq_count = lax.axis_size("freq")
    spread = farm(
        cols, prior_seeds[0], window_seeds[0], places(depth * parts, window), spectra, nugget,
        decay.reshape(1, 1), parts, lax.axis_size("col"), freq_count,
    )
    return synthesize(spread).reshape(2 * spread.shape[2], spread.shape[3], STEPS)


def solution(mesh):
    in_specs = (
        P("freq", ("row", "col"), None),
        P("freq", ("row", "col"), None),
        P("freq", None, None),
        P("freq", None),
        P("freq", None),
        P("freq"),
    )
    out_specs = P("freq", ("row", "col"), None)
    return jax.shard_map(shards, mesh=mesh, in_specs=in_specs, out_specs=out_specs, check_vma=False)
```
